512 devices in a mesh: pipe: 16 (over z_hi, y), dp: 32 (over x, z_lo, core).
Axes of the slice: x: 4, y: 4, z: 16 (z_hi: 4, z_lo: 4; z = z_hi * 4 + z_lo), core: 2. Of those that a mesh axis runs over, the one named last changes fastest.
Arguments:
- episode_states: bfloat16 [2, 2, 1024, 896], P(None, None, 'dp'), may hold values from -200 to 200
- norm_gain: bfloat16 [16, 896], P('pipe', 'dp'), may hold values from 0.099609375 to 1.8984375
- qkv_weight: bfloat16 [16, 896, 576], P('pipe', 'dp'), may hold values from -10 to 10
- out_weight: bfloat16 [16, 448, 896], P('pipe', 'dp'), may hold values from -0.25 to 0.25
- final_gain: bfloat16 [896], replicated, may hold values from 0.099609375 to 1.8984375
- value_weight: bfloat16 [896], replicated, may hold values from -0.1875 to 0.1875
- target_positions: int32 [2, 2, 32, 16], P(None, None, 'dp'), may hold values from 0 to 31
- value_targets: float32 [2, 2, 32, 16], P(None, None, 'dp'), may hold values from -4 to 4
Outputs:
- grad_gain: float32 [16, 896], P('pipe', 'dp')
- grad_qkv: float32 [16, 896, 576], P('pipe', 'dp')
- grad_out: float32 [16, 448, 896], P('pipe', 'dp')
The draws below stay inside these ranges and needn't reach their ends.
Inputs may be any that keep to these rules, and one draw needn't show every extreme that they name: `target_positions`: positions inside one window of 32 tokens; a position may appear more than once.
All inputs are finite; a program needn't handle non-finite values.
Results may differ from the reference program's by a relative error of at most 0.035.
Values may be sent and summed in bfloat16 or wider, within the bound.
A program may use at most 64 MiB of HBM per device.

```python
import math
import jax
import jax.numpy as jnp
from jax import lax

D = 896
HEAD = 64
QHEADS = 7
MICRO = 2
ROWS = 32
TARGETS = 16
QDIM = 448
QKV = 576
SECTIONS = 16
EPIROWS = 1024
N_DP = 32


def draw_episode_states(key, part):
    key_main = jax.random.fold_in(key, 0)
    full_shape = (2, MICRO, EPIROWS, D)
    drawn = jnp.clip(jax.random.normal(key_main, full_shape, jnp.float32), -6.0, 6.0)
    return drawn.astype(jnp.bfloat16)


def draw_qkv_weight(key, part):
    key_main = jax.random.fold_in(key, 0)
    drawn = jnp.clip(jax.random.normal(key_main, (SECTIONS, D, QKV), jnp.float32), -6.0, 6.0) * D ** (-0.5)
    return drawn.astype(jnp.bfloat16)


def place_ends(values, stream_key, low, high):
    shape = values.shape
    spot = [jax.random.randint(jax.random.fold_in(stream_key, axis), (), 0, shape[axis]) for axis in range(len(shape))]
    values = values.at[tuple(spot)].set(low)
    longest = shape.index(max(shape))
    spot[longest] = (spot[longest] + 1) % shape[longest]
    return values.at[tuple(spot)].set(high)


def shard_levels(stream_key, extent, cuts, smallest, largest):
    def one(dim, shards_of):
        draws = jax.random.uniform(jax.random.fold_in(jax.random.fold_in(stream_key, 6), dim), (shards_of,), jnp.float32, smallest / len(cuts), largest / len(cuts))
        return jnp.repeat(jnp.exp(draws), extent[dim] // shards_of).reshape((-1,) + (1,) * (len(extent) - dim - 1))

    gain = one(*cuts[0])
    for cut in cuts[1:]:
        gain = gain * one(*cut)
    return gain


def normal_values(rng, shape, scale, reach, pieces=(), held_as=jnp.bfloat16):
    level = shard_levels(rng, shape, pieces, -0.22, 0.18) if pieces else 1.0
    result = jax.random.normal(rng, shape, jnp.float32) * scale * level
    return jnp.minimum(jnp.maximum(result, -reach), reach).astype(held_as)


def setup_inputs(seed: int = 0) -> dict:
    arg_keys = jax.random.split(jax.random.key(seed), 9)
    return {
        "episode_states": draw_episode_states(jax.random.fold_in(arg_keys[8], 71), 0),
        "norm_gain": jnp.clip(1.0 + 0.18 * jax.random.normal(arg_keys[1], (SECTIONS, D), jnp.float32), 0.099609375, 1.8984375).astype(jnp.bfloat16),
        "qkv_weight": draw_qkv_weight(jax.random.fold_in(arg_keys[8], 71), 0),
        "out_weight": normal_values(arg_keys[3], (SECTIONS, QDIM, D), QDIM ** -0.5, 0.25, ((0, 16), (1, 32))),
        "final_gain": jnp.clip(1.0 + 0.18 * jax.random.normal(arg_keys[4], (D,), jnp.float32), 0.099609375, 1.8984375).astype(jnp.bfloat16),
        "value_weight": normal_values(arg_keys[5], (D,), D ** -0.5, 0.1875),
        "target_positions": place_ends(jax.random.randint(arg_keys[6], (2, MICRO, N_DP, TARGETS), 0, ROWS), jax.random.fold_in(arg_keys[6], 1), 0, ROWS - 1).astype(jnp.int32),
        "value_targets": normal_values(arg_keys[7], (2, MICRO, N_DP, TARGETS), 1.0, 4.0, ((2, 32),), jnp.float32),
    }


def section_apply(states, norm_scale, qkv_mat, out_mat):
    row_count = states.shape[0]
    query_width = QHEADS * HEAD
    widened = states.astype(jnp.float32)
    inverse_rms = lax.rsqrt(lax.optimization_barrier(jnp.mean(widened * widened, axis=-1, keepdims=True)) + 1e-06)
    normed = (widened * inverse_rms * norm_scale.astype(jnp.float32)).astype(jnp.bfloat16)
    projected = jnp.dot(normed, qkv_mat, preferred_element_type=jnp.float32).astype(jnp.bfloat16)
    queries = projected[:, :query_width].reshape(row_count, QHEADS, HEAD).astype(jnp.float32)
    key_rows = projected[:, query_width:query_width + HEAD].astype(jnp.float32)
    value_rows = projected[:, query_width + HEAD:].astype(jnp.float32)
    scores = jnp.einsum('qhd,kd->hqk', queries, key_rows) * (1.0 / math.sqrt(HEAD))
    position = jnp.arange(row_count, dtype=jnp.int32)
    allowed = position[:, None] >= position[None, :]
    scores = jnp.where(allowed[None, :, :], scores, -1e+30)
    row_max = lax.optimization_barrier(jnp.max(scores, axis=-1, keepdims=True))
    weights = jnp.exp(scores - row_max)
    attention = (weights / lax.optimization_barrier(jnp.sum(weights, axis=-1, keepdims=True))).astype(jnp.bfloat16)
    attended = jnp.einsum('hqk,kd->qhd', attention.astype(jnp.float32), value_rows)
    attended = attended.astype(jnp.bfloat16).reshape(row_count, query_width)
    update = jnp.dot(attended, out_mat, preferred_element_type=jnp.float32)
    return (widened + update).astype(jnp.bfloat16)

def value_loss(final_states, final_scale, head_weight, chosen, wanted):
    widened = final_states.astype(jnp.float32)
    inverse_rms = lax.rsqrt(lax.optimization_barrier(jnp.mean(widened * widened, axis=-1, keepdims=True)) + 1e-06)
    predicted = lax.optimization_barrier(jnp.sum(widened * inverse_rms * final_scale.astype(jnp.float32) * head_weight.astype(jnp.float32), axis=-1))
    selector = (chosen[:, None] == jnp.arange(final_states.shape[0], dtype=jnp.int32)[None, :]).astype(jnp.float32)
    picked = lax.optimization_barrier(jnp.sum(selector * predicted[None, :], axis=-1))
    residual = picked - wanted
    return 0.5 * jnp.sum(residual * residual)

def section_pullback(states, cotangent, norm_scale, qkv_mat, out_mat):
    unused, pullback = jax.vjp(section_apply, states, norm_scale, qkv_mat, out_mat)
    return pullback(cotangent)

def reference(episode_states, norm_gain, qkv_weight, out_weight, final_gain, value_weight, target_positions, value_targets):
    running_totals = [jnp.zeros((SECTIONS, D), jnp.float32), jnp.zeros((SECTIONS, D, QKV), jnp.float32), jnp.zeros((SECTIONS, QDIM, D), jnp.float32)]
    forward_section = jax.vmap(section_apply, in_axes=(0, None, None, None))
    backward_section = jax.vmap(section_pullback, in_axes=(0, 0, None, None, None))
    loss_grad = jax.vmap(jax.grad(value_loss), in_axes=(0, None, None, 0, 0))
    for copy_index in range(2):
        current = episode_states[copy_index].reshape(MICRO * N_DP, ROWS, D)
        inputs_saved = []
        for section_index in range(SECTIONS):
            inputs_saved.append(current)
            current = forward_section(current, norm_gain[section_index], qkv_weight[section_index], out_weight[section_index])
        chosen = target_positions[copy_index].reshape(MICRO * N_DP, TARGETS).astype(jnp.int32)
        wanted = value_targets[copy_index].reshape(MICRO * N_DP, TARGETS)
        cotangent = loss_grad(current, final_gain, value_weight, chosen, wanted)
        for section_index in reversed(range(SECTIONS)):
            pulled = backward_section(inputs_saved[section_index], cotangent, norm_gain[section_index], qkv_weight[section_index], out_weight[section_index])
            cotangent = pulled[0]
            updated = []
            for running, increment in zip(running_totals, pulled[1:]):
                per_window = increment.reshape((MICRO, N_DP) + increment.shape[1:]).astype(jnp.float32)
                partial_sum = lax.optimization_barrier(lax.optimization_barrier(jnp.sum(per_window, axis=0)).astype(jnp.bfloat16)).astype(jnp.float32)
                updated.append(running.at[section_index].add(lax.optimization_barrier(jnp.sum(partial_sum, axis=0))))
            running_totals = updated
    return (running_totals[0], running_totals[1], running_totals[2])
```

```python
import functools
import math

import jax
import jax.numpy as jnp
from jax import lax
from jax.experimental import pallas as pl
from jax.experimental.pallas import tpu as pltpu
from jax.sharding import PartitionSpec as P

MESH = pl.DeviceIdType.MESH
HEAD = 64
QHEADS = 7
QDIM = HEAD * QHEADS
QKV = QDIM + 2 * HEAD
D = 896
ROWS = 32
CORES = 2
EPS = 1e-06
F32 = jnp.float32
BF16 = jnp.bfloat16
NT = (((1,), (1,)), ((), ()))
TN = (((0,), (0,)), ((), ()))


def dot(a, b, dims=None):
    if dims is None:
        return jnp.dot(a, b, preferred_element_type=F32)
    return lax.dot_general(a, b, dims, preferred_element_type=F32)


def low_half():
    return lax.broadcasted_iota(jnp.int32, (ROWS, 128), 1) < HEAD


def stack_heads(tiles):
    low = low_half()
    parts = []
    for head in range(QHEADS):
        tile = tiles[head // 2]
        parts.append(jnp.where(low if head % 2 == 0 else ~low, tile, 0.0))
    return jnp.concatenate(parts, axis=0).astype(BF16)


def unstack_heads(stacked, last):
    low = low_half()
    tiles = []
    for pair in range(QHEADS // 2):
        base = pair * 2 * ROWS
        tiles.append(jnp.where(low, stacked[base : base + ROWS], stacked[base + ROWS : base + 2 * ROWS]))
    tiles.append(jnp.where(low, stacked[6 * ROWS : 7 * ROWS], last))
    return tiles


def both_halves(tile, from_low):
    turned = pltpu.roll(tile, HEAD, 1)
    low = low_half()
    return jnp.where(low, tile, turned) if from_low else jnp.where(low, turned, tile)


def widen(tile):
    return jnp.concatenate([tile, jnp.zeros_like(tile)], axis=1)


def relay_kernel(
    geo,
    states_ref,
    wq_sh,
    wo_sh,
    fg_ref,
    vw_ref,
    pos_ref,
    want_ref,
    gq_out,
    go_out,
    dg_out,
    bq,
    bo,
    tq,
    to,
    wqf,
    wof,
    gp,
    gs,
    xs,
    ns,
    qst,
    kd,
    vd,
    ps,
    at,
    rr,
    cs,
    dps,
    gq,
    go,
    rq0,
    ro0,
    r1q,
    r1o,
    so,
    r2q,
    r2o,
    sq3,
    so3,
    r3q,
    r3o,
    fq,
    fo,
    dg,
    dgr,
    ss,
    rs,
):
    nst, ny, nx, nz = geo
    nc = CORES
    ndp = nx * nz * nc
    rq, ro = D // ndp, QDIM // ndp
    gqr, gor = D // nx, QDIM // nx
    p, d = lax.axis_index("pipe"), lax.axis_index("dp")
    div, rem = lax.div, lax.rem
    stage, y = div(p, ny), rem(p, ny)
    x, z, c = div(d, nz * nc), rem(div(d, nc), nz), rem(d, nc)
    slots = {}

    def slot(*name):
        return slots.setdefault(name, len(slots))

    def rcopy(src, dst, name, dev):
        i = slot(*name)
        return pltpu.make_async_remote_copy(
            src_ref=src,
            dst_ref=dst,
            send_sem=ss.at[i],
            recv_sem=rs.at[i],
            device_id=dev,
            device_id_type=MESH,
        )

    def dpi(xx, zz, cc):
        return (xx * nz + zz) * nc + cc

    partner = (p, dpi(x, z, 1 - c))
    zdev = [(p, dpi(x, rem(z + t, nz), c)) for t in range(nz)]
    xdev = [(p, dpi(rem(x + t, nx), z, c)) for t in range(nx)]
    ydev = [(stage * ny + rem(y + t, ny), d) for t in range(ny)]
    nextdev = (rem(stage + 1, nst) * ny + y, d)
    prevdev = (rem(stage + nst - 1, nst) * ny + y, d)
    zf = [rem(z + nz - t, nz) for t in range(nz)]
    zt = [rem(z + t, nz) for t in range(nz)]
    xf_ = [rem(x + nx - t, nx) for t in range(nx)]
    xt_ = [rem(x + t, nx) for t in range(nx)]
    yf_ = [rem(y + ny - t, ny) for t in range(ny)]
    yt_ = [rem(y + t, ny) for t in range(ny)]
    pending = []

    def V(ref, *place):
        return ref, place

    def view(spot):
        ref, place = spot
        return ref.at[place] if place else ref

    def send(src, dst, name, dev, group="all"):
        make = lambda: rcopy(view(src), view(dst), name, dev)
        make().start()
        pending.append((group, make))

    def recv(ref, name):
        rcopy(view(ref), view(ref), name, partner).wait_recv()

    def starts(places, size):
        return [pl.ds(pl.multiple_of(place * size, 16), size) for place in places]

    q_from, q_to = starts(xf_, gqr), starts(xt_, gqr)
    o_from, o_to = starts(xf_, gor), starts(xt_, gor)

    peers = [partner] + zdev[1:] + xdev[1:] + ydev[1:]
    if nst > 1:
        peers = peers + [nextdev, prevdev]
    barrier = pltpu.get_barrier_semaphore()
    for dev in peers:
        pl.semaphore_signal(barrier, inc=1, device_id=dev, device_id_type=MESH)
    pl.semaphore_wait(barrier, len(peers))

    i_me = z * nc + c
    for t in range(1, nz):
        send(V(wq_sh), V(bq, i_me), ("zq", t), zdev[t])
        send(V(wo_sh), V(bo, i_me), ("zo", t), zdev[t])
    send(V(wq_sh), V(bq, i_me), ("pq", 0), partner)
    send(V(wo_sh), V(bo, i_me), ("po", 0), partner)
    bq[i_me] = wq_sh[...]
    bo[i_me] = wo_sh[...]
    for t in range(1, nz):
        i_f = zf[t] * nc + c
        recv(V(bq, i_f), ("zq", t))
        send(V(bq, i_f), V(bq, i_f), ("pq", t), partner)
        recv(V(bo, i_f), ("zo", t))
        send(V(bo, i_f), V(bo, i_f), ("po", t), partner)
    for t in range(nz):
        i_f = zf[t] * nc + 1 - c
        recv(V(bq, i_f), ("pq", t))
        recv(V(bo, i_f), ("po", t))

    @pl.when(c == 0)
    def _():
        for i in range(nz * nc):
            tq[rq * i : rq * (i + 1), :] = bq[i].astype(F32)
        wqf[y, q_to[0], :] = tq[...].astype(BF16)
        mine = V(wqf, y, q_to[0])
        for t in range(1, nx):
            send(mine, mine, ("xq", t), xdev[t], "c0")
        for t in range(1, nx):
            recv(V(wqf, y, q_from[t]), ("xq", t))
        for t in range(1, ny):
            send(V(wqf, y), V(wqf, y), ("yq", t), ydev[t], "c0")
        send(V(wqf, y), V(wqf, y), ("fq", 0), partner, "c0")
        for t in range(1, ny):
            recv(V(wqf, yf_[t]), ("yq", t))
            send(V(wqf, yf_[t]), V(wqf, yf_[t]), ("fq", t), partner, "c0")
        for t in range(nx):
            recv(V(wof, pl.ds(0, ny), o_from[t]), ("fo", t))
            recv(V(gp, pl.ds(0, ny), xf_[t]), ("fg", t))

    @pl.when(c == 1)
    def _():
        gain = jnp.zeros((1, D), F32)
        for i in range(nz * nc):
            shard = bo[i].astype(F32)
            to[ro * i : ro * (i + 1), :] = shard[0:ro]
            gain = gain + shard[ro : ro + 1]
        wof[y, o_to[0], :] = to[...].astype(BF16)
        gp[y, x] = jnp.broadcast_to(gain, (8, D))
        mine = V(wof, y, o_to[0])
        for t in range(1, ny):
            send(mine, mine, ("yo", t), ydev[t], "c1")
            send(V(gp, y, x), V(gp, y, x), ("yg", t), ydev[t], "c1")
        for t in range(1, ny):
            recv(V(wof, yf_[t], o_to[0]), ("yo", t))
            recv(V(gp, yf_[t], x), ("yg", t))

        def block(t):
            return V(wof, pl.ds(0, ny), o_from[t])

        for t in range(1, nx):
            send(block(0), block(0), ("xo", t), xdev[t], "c1")
            send(V(gp, pl.ds(0, ny), x), V(gp, pl.ds(0, ny), x), ("xg", t), xdev[t], "c1")
        send(block(0), block(0), ("fo", 0), partner, "c1")
        send(V(gp, pl.ds(0, ny), x), V(gp, pl.ds(0, ny), x), ("fg", 0), partner, "c1")
        for t in range(1, nx):
            recv(block(t), ("xo", t))
            send(block(t), block(t), ("fo", t), partner, "c1")
            recv(V(gp, pl.ds(0, ny), xf_[t]), ("xg", t))
            send(V(gp, pl.ds(0, ny), xf_[t]), V(gp, pl.ds(0, ny), xf_[t]), ("fg", t), partner, "c1")
        for t in range(ny):
            recv(V(wqf, yf_[t]), ("fq", t))

    for k in range(ny):
        total = gp[k, 0]
        for xx in range(1, nx):
            total = total + gp[k, xx]
        gs[k] = total
    dg[...] = jnp.zeros_like(dg)

    @pl.when(stage == 0)
    def _():
        xs[0] = states_ref[y]

    if nst > 1:

        @pl.when(stage > 0)
        def _():
            recv(V(xs, 0), ("hop",))

    def forward(k, carry):
        wide = xs[k].astype(F32)
        r = lax.rsqrt(jnp.sum(wide * wide, axis=-1, keepdims=True) * (1.0 / D) + EPS)
        rr[k] = jnp.broadcast_to(r, (ROWS, 128))
        normed = (wide * r * gs[k, 0:1, :]).astype(BF16)
        ns[k] = normed
        projected = dot(normed, wqf[k]).astype(BF16).astype(F32)
        tiles = [projected[:, 128 * i : 128 * (i + 1)] for i in range(4)]
        queries = stack_heads(tiles)
        keys = both_halves(tiles[3], False).astype(BF16)
        values = both_halves(widen(projected[:, 4 * 128 :]), True).astype(BF16)
        qst[k], kd[k], vd[k] = queries, keys, values
        scores = dot(keys, queries, NT) * (1.0 / math.sqrt(HEAD))
        key_at = lax.broadcasted_iota(jnp.int32, scores.shape, 0)
        query_at = lax.broadcasted_iota(jnp.int32, scores.shape, 1) & (ROWS - 1)
        scores = jnp.where(query_at >= key_at, scores, -1e30)
        weights = jnp.exp(scores - jnp.max(scores, axis=0, keepdims=True))
        attention = weights / jnp.sum(weights, axis=0, keepdims=True)
        ps[k] = attention
        attended = unstack_heads(dot(attention.astype(BF16), values, TN), 0.0)
        attended = jnp.concatenate(attended[:3] + [attended[3][:, :HEAD]], axis=1).astype(BF16)
        at[k] = attended
        xs[k + 1] = (wide + dot(attended, wof[k])).astype(BF16)
        return carry

    lax.fori_loop(0, ny, forward, 0)

    if nst > 1:

        @pl.when(stage < nst - 1)
        def _():
            send(V(xs, ny), V(xs, 0), ("hop",), nextdev, "up")

    @pl.when(stage == nst - 1)
    def _():
        wide = xs[ny].astype(F32)
        w = fg_ref[...].astype(F32) * vw_ref[...].astype(F32)
        r = lax.rsqrt(jnp.sum(wide * wide, axis=-1, keepdims=True) * (1.0 / D) + EPS)
        predicted = r * jnp.sum(wide * w, axis=-1, keepdims=True)
        chosen = pos_ref[pl.ds(y, 1), :]
        wanted = want_ref[pl.ds(y, 1), :]
        at_row = lax.broadcasted_iota(jnp.int32, (ROWS, chosen.shape[1]), 0)
        selector = (at_row == chosen).astype(F32)
        residual = jnp.sum(selector * predicted, axis=0, keepdims=True) - wanted
        slope = jnp.sum(selector * residual, axis=1, keepdims=True)
        cs[ny] = (slope * (r * w - wide * (r * r * predicted * (1.0 / D)))).astype(BF16)

    if nst > 1:

        @pl.when(stage < nst - 1)
        def _():
            recv(V(cs, ny), ("back",))

    def backward(step, carry):
        k = ny - 1 - step
        cot = cs[k + 1]
        d_att = dot(cot, wof[k], NT)
        tiles = [d_att[:, 128 * i : 128 * (i + 1)] for i in range(3)] + [widen(d_att[:, 3 * 128 :])]
        stacked = stack_heads(tiles)
        attention = ps[k]
        d_attention = dot(vd[k], stacked, NT)
        inner = jnp.sum(d_attention * attention, axis=0, keepdims=True)
        d_scores = (attention * (d_attention - inner) * (1.0 / math.sqrt(HEAD))).astype(BF16)
        d_values = dot(attention.astype(BF16), stacked)
        d_keys = dot(d_scores, qst[k])
        d_queries = dot(d_scores, kd[k], TN)
        d_values = d_values + pltpu.roll(d_values, HEAD, 1)
        d_keys = d_keys + pltpu.roll(d_keys, HEAD, 1)
        d_proj = unstack_heads(d_queries, d_keys) + [d_values[:, :HEAD]]
        d_proj = jnp.concatenate(d_proj, axis=1).astype(BF16)
        dps[k] = d_proj
        d_normed = dot(d_proj, wqf[k], NT)
        wide = xs[k].astype(F32)
        r = rr[k][:, 0:1]
        unit = wide * r
        dg[pl.ds(k, 1), :] = jnp.sum(d_normed * unit, axis=0, keepdims=True)
        scaled = d_normed * gs[k, 0:1, :]
        mean = jnp.sum(scaled * unit, axis=-1, keepdims=True) * (1.0 / D)
        cs[k] = (cot.astype(F32) + r * (scaled - unit * mean)).astype(BF16)
        return carry

    lax.fori_loop(0, ny, backward, 0)

    if nst > 1:

        @pl.when(stage > 0)
        def _():
            send(V(cs, 0), V(cs, ny), ("back",), prevdev, "down")

    def weight_grads(k):
        gq[k] = dot(ns[k], dps[k], TN).astype(BF16)
        go[k] = dot(at[k], cs[k + 1], TN).astype(BF16)

    order = [t for t in range(1, ny)] + [0]

    def hand_over(t):
        k = yt_[t]

        @pl.when(c == 0)
        def _():
            send(V(go, k), V(ro0, k), ("r0", t), partner, "c0")

        @pl.when(c == 1)
        def _():
            send(V(gq, k), V(rq0, k), ("r0q", t), partner, "c1")

    def pass_on(t):
        k = yt_[t]

        @pl.when(c == 0)
        def _():
            recv(V(rq0, k), ("r0q", t))

            @pl.loop(0, D // 112)
            def _(i):
                rows = pl.ds(pl.multiple_of(i * 112, 16), 112)
                gq[k, rows, :] = (gq[k, rows, :].astype(F32) + rq0[k, rows, :].astype(F32)).astype(BF16)

            if t:
                send(V(gq, k), V(r1q, t - 1), ("r1q", t), ydev[t], "c0")

        @pl.when(c == 1)
        def _():
            recv(V(ro0, k), ("r0", t))

            @pl.loop(0, QDIM // 112)
            def _(i):
                rows = pl.ds(pl.multiple_of(i * 112, 16), 112)
                go[k, rows, :] = (go[k, rows, :].astype(F32) + ro0[k, rows, :].astype(F32)).astype(BF16)

            for u in range(1, nx):
                send(V(go, k, o_to[u]), V(r1o, u - 1, k), ("r1o", t, u), xdev[u], "c1")

    @pl.when(c == 0)
    def _():
        send(V(dg), V(dgr, 0), ("dg0",), partner, "c0")

    before = None
    for t in order:
        weight_grads(yt_[t])
        hand_over(t)
        if before is not None:
            pass_on(before)
        before = t
    pass_on(before)

    @pl.when(c == 0)
    def _():
        for t in range(1, ny):
            recv(V(r1q, t - 1), ("r1q", t))

        @pl.loop(0, D // 112)
        def _(i):
            rows = pl.ds(pl.multiple_of(i * 112, 16), 112)
            total = gq[y, rows, :].astype(F32)
            for t in range(1, ny):
                total = total + r1q[t - 1, rows, :].astype(F32)
            rq0[y, rows, :] = total.astype(BF16)

        for t in range(1, nx):
            send(V(rq0, y, q_to[t]), V(r2q, t - 1), ("r2q", t), xdev[t], "c0")
        for t in range(1, nx):
            recv(V(r2q, t - 1), ("r2q", t))
        total = rq0[y, q_to[0], :].astype(F32)
        for t in range(1, nx):
            total = total + r2q[t - 1].astype(F32)
        tq[...] = total
        for i in range(nz * nc):
            sq3[i // nc, i % nc] = tq[rq * i : rq * (i + 1), :].astype(BF16)
        for t in range(1, nz):
            send(V(sq3, zt[t]), V(r3q, t - 1), ("r3q", t), zdev[t], "c0")
        for t in range(1, nz):
            recv(V(r3q, t - 1), ("r3q", t))
        for cc in range(nc):
            total = sq3[z, cc].astype(F32)
            for t in range(1, nz):
                total = total + r3q[t - 1, cc].astype(F32)
            if cc == 0:
                gq_out[...] = total
            else:
                fq[0] = total
        send(V(fq, 0), V(fq, 1), ("f4q",), partner, "c0")
        recv(V(fo, 1), ("f4o",))
        go_out[...] = fo[1]
        recv(V(dgr, 1), ("dg4",))
        dg_out[...] = dgr[1]

    @pl.when(c == 1)
    def _():
        recv(V(dgr, 0), ("dg0",))
        gains = dg[...] + dgr[0]
        dgr[2] = gains
        for t in range(1, nx):
            send(V(dgr, 2), V(dgr, 5 + t), ("dgx", t), xdev[t], "c1")
        for k in range(ny):
            base = go[k, o_to[0], :].astype(F32)
            so[k] = base
        for u in range(ny):
            k = yt_[u]
            for t in range(1, nx):
                recv(V(r1o, t - 1, yt_[u]), ("r1o", u, t))
            total = so[k]
            for t in range(1, nx):
                total = total + r1o[t - 1, k].astype(F32)
            ro0[k, 0:gor, :] = total.astype(BF16)
            if u:
                send(V(ro0, k, pl.ds(0, gor)), V(r2o, u - 1), ("r2o", u), ydev[u], "c1")
        for t in range(1, nx):
            recv(V(dgr, 5 + t), ("dgx", t))
            gains = gains + dgr[5 + t]
        dgr[3] = gains
        for t in range(1, ny):
            send(V(dgr, 3), V(dgr, 8 + t), ("dgy", t), ydev[t], "c1")
        for t in range(1, ny):
            recv(V(r2o, t - 1), ("r2o", t))
        total = ro0[y, 0:gor, :].astype(F32)
        for t in range(1, ny):
            total = total + r2o[t - 1].astype(F32)
        to[...] = total
        for i in range(nz * nc):
            so3[i // nc, i % nc] = to[ro * i : ro * (i + 1), :].astype(BF16)
        for t in range(1, nz):
            send(V(so3, zt[t]), V(r3o, t - 1), ("r3o", t), zdev[t], "c1")
        for t in range(1, ny):
            recv(V(dgr, 8 + t), ("dgy", t))
            gains = gains + dgr[8 + t]
        dgr[4] = gains
        for t in range(1, nz):
            send(V(dgr, 4), V(dgr, 11 + t), ("dgz", t), zdev[t], "c1")
        for t in range(1, nz):
            recv(V(r3o, t - 1), ("r3o", t))
        for cc in range(nc):
            total = so3[z, cc].astype(F32)
            for t in range(1, nz):
                total = total + r3o[t - 1, cc].astype(F32)
            if cc == 1:
                go_out[...] = total
            else:
                fo[0] = total
        send(V(fo, 0), V(fo, 1), ("f4o",), partner, "c1")
        for t in range(1, nz):
            recv(V(dgr, 11 + t), ("dgz", t))
            gains = gains + dgr[11 + t]
        dgr[5] = gains
        send(V(dgr, 5), V(dgr, 1), ("dg4",), partner, "c1")
        dg_out[...] = gains
        recv(V(fq, 1), ("f4q",))
        gq_out[...] = fq[1]

    conditions = {"all": None, "c0": c == 0, "c1": c == 1, "up": stage < nst - 1, "down": stage > 0}
    for group, condition in conditions.items():
        makers = [make for name, make in pending if name == group]
        if not makers:
            continue
        if condition is None:
            for make in makers:
                make().wait_send()
        else:

            @pl.when(condition)
            def _():
                for make in makers:
                    make().wait_send()


def scratch(geo):
    nst, ny, nx, nz = geo
    nc = CORES
    ndp = nx * nz * nc
    rq, ro = D // ndp, QDIM // ndp
    rop = -(-(ro + 1) // 16) * 16
    gqr, gor = D // nx, QDIM // nx
    v = pltpu.VMEM
    return [
        v((nz * nc, rq, QKV), BF16),
        v((nz * nc, rop, D), BF16),
        v((gqr, QKV), F32),
        v((gor, D), F32),
        v((ny, D, QKV), BF16),
        v((ny, QDIM, D), BF16),
        v((ny, nx, 8, D), F32),
        v((ny, 8, D), F32),
        v((ny + 1, ROWS, D), BF16),
        v((ny, ROWS, D), BF16),
        v((ny, QHEADS * ROWS, 128), BF16),
        v((ny, ROWS, 128), BF16),
        v((ny, ROWS, 128), BF16),
        v((ny, ROWS, QHEADS * ROWS), F32),
        v((ny, ROWS, QDIM), BF16),
        v((ny, ROWS, 128), F32),
        v((ny + 1, ROWS, D), BF16),
        v((ny, ROWS, QKV), BF16),
        v((ny, D, QKV), BF16),
        v((ny, QDIM, D), BF16),
        v((ny, D, QKV), BF16),
        v((ny, QDIM, D), BF16),
        v((max(ny - 1, 1), D, QKV), BF16),
        v((max(nx - 1, 1), ny, gor, D), BF16),
        v((ny, gor, D), F32),
        v((max(nx - 1, 1), gqr, QKV), BF16),
        v((max(ny - 1, 1), gor, D), BF16),
        v((nz, nc, rq, QKV), BF16),
        v((nz, nc, ro, D), BF16),
        v((max(nz - 1, 1), nc, rq, QKV), BF16),
        v((max(nz - 1, 1), nc, ro, D), BF16),
        v((2, rq, QKV), F32),
        v((2, ro, D), F32),
        v((8, D), F32),
        v((15, 8, D), F32),
        pltpu.SemaphoreType.DMA((96,)),
        pltpu.SemaphoreType.DMA((96,)),
    ]


def per_device(geo, states, norm_gain, qkv_weight, out_weight, final_gain, value_weight, positions, targets):
    nst, ny, nx, nz = geo
    ndp = nx * nz * CORES
    rq, ro = D // ndp, QDIM // ndp
    rop = -(-(ro + 1) // 16) * 16
    d = lax.axis_index("dp")
    y = lax.axis_index("pipe") % ny
    lanes = lax.broadcasted_iota(jnp.int32, (ndp, rq), 0)
    gain_row = jnp.where(lanes == d, norm_gain, 0).reshape(1, D)
    wo = jnp.concatenate([out_weight[0], gain_row, jnp.zeros((rop - ro - 1, D), BF16)], axis=0)
    windows = states.shape[0] * states.shape[1]
    vmem = pl.BlockSpec(memory_space=pltpu.VMEM)
    gq, go, dg = pl.pallas_call(
        functools.partial(relay_kernel, geo),
        out_shape=(
            jax.ShapeDtypeStruct((rq, QKV), F32),
            jax.ShapeDtypeStruct((ro, D), F32),
            jax.ShapeDtypeStruct((8, D), F32),
        ),
        in_specs=[vmem] * 7,
        out_specs=(vmem, vmem, vmem),
        scratch_shapes=scratch(geo),
        compiler_params=pltpu.CompilerParams(
            collective_id=0, has_side_effects=True, vmem_limit_bytes=56 * 1024 * 1024
        ),
        name="relay",
    )(
        states.reshape(windows, ROWS, D),
        qkv_weight[0],
        wo,
        final_gain.reshape(1, D),
        value_weight.reshape(1, D),
        positions.reshape(windows, -1),
        targets.reshape(windows, -1),
    )
    grad_gain = lax.dynamic_slice(dg, (y, d * rq), (1, rq))
    return grad_gain, gq[None], go[None]


def solution(mesh, geo=(4, 4, 4, 4)):
    return jax.shard_map(
        functools.partial(per_device, geo),
        mesh=mesh,
        in_specs=(
            P(None, None, "dp", None),
            P("pipe", "dp"),
            P("pipe", "dp", None),
            P("pipe", "dp", None),
            P(),
            P(),
            P(None, None, "dp", None),
            P(None, None, "dp", None),
        ),
        out_specs=(P("pipe", "dp"), P("pipe", "dp", None), P("pipe", "dp", None)),
        check_vma=False,
    )
```
